32 devices in a mesh: group: 2 (over core), local: 16 (over z, y, x).
Axes of the slice: x: 2, y: 2, z: 4, core: 2. Of those that a mesh axis runs over, the one named last changes fastest.
Arguments:
- features: bfloat16 [64, 32, 1728], P(('group', 'local')), may hold values from -6 to 6
- neighbours: int32 [64, 27], P(('group', 'local')), may hold values from -1 to 1, as said below
- coarse_dest: int32 [64], P(('group', 'local')), may hold values from -1 to 3, as said below
- weight_first: bfloat16 [32, 864], replicated, may hold values from -0.21875 to 0.21875
- bias_first: float32 [32], replicated, may hold values from -3 to 3
- reduce_weight: bfloat16 [64, 256], replicated, may hold values from -0.375 to 0.375
- reduce_bias: float32 [64], replicated, may hold values from -3 to 3
- weight_coarse: bfloat16 [64, 1728], replicated, may hold values from -0.15625 to 0.15625
- bias_coarse: float32 [64], replicated, may hold values from -3 to 3
- weight_up: bfloat16 [32, 64], replicated, may hold values from -0.75 to 0.75
- bias_up: float32 [32], replicated, may hold values from -3 to 3
- weight_last: bfloat16 [32, 1728], replicated, may hold values from -0.15625 to 0.15625
- bias_last: float32 [32], replicated, may hold values from -3 to 3
Outputs:
- decoded: bfloat16 [64, 32, 1728], P(('group', 'local'))
- balanced_coarse: bfloat16 [128, 64, 216], P(('group', 'local'))
The draws below stay inside these ranges and needn't reach their ends.
Inputs may be any that keep to these rules, and one draw needn't show every extreme that they name: `neighbours`: both slots of every device are live. For a live slot, entry (dx + 1) * 9 + (dy + 1) * 3 + dz + 1 names the live slot of the device with the same group index and local index l + dx that holds the block at offset (dx, dy, dz), or -1 where that block is absent or lies outside the group; entry 13 is the slot itself. The blocks of one device form one layer of blocks along the first dimension, the next local index holding the next layer. `coarse_dest`: -1 exactly for empty slots; else r * 2 + k, naming slot k of the coarse cubes that this device sends to the device of the same local index in group r. No two slots of a device share a value; in every draw some device sends 2 cubes to one group.
All inputs are finite; a program needn't handle non-finite values.
Results may differ from the reference program's by a relative error of at most 0.0049.
Values may be sent and summed in bfloat16 or wider, within the bound.
A program may use at most 64 MiB of HBM per device.

```python
import math
import jax
import jax.numpy as jnp
from jax import lax

C = 32
CC = 64
SIDE = 12
SEND_CAP = 2
CAP = 2
BLOCKS = 64
BAL_SLOTS = 128
N_GROUP = 2
N_LOCAL = 16


def layout(key):
    base_key = jax.random.fold_in(key, 4099)
    key_base, key_jitter, key_place, key_offset = jax.random.split(base_key, 4)
    grid_side = int(math.ceil(math.sqrt(CAP)))
    base_count = jax.random.randint(key_base, (N_GROUP, 1), max(CAP - 1, 2), CAP + 1)
    jitter = jax.random.randint(key_jitter, (N_GROUP, N_LOCAL), -1, 2)
    live_count = jnp.clip(base_count + jitter, 2, CAP)
    live_count = live_count.at[0, 0].set(CAP).at[N_GROUP - 1, N_LOCAL - 1].set(2)
    device_keys = jax.random.split(key_place, N_GROUP * N_LOCAL)
    places = jax.vmap(lambda device_key: jax.random.permutation(device_key, grid_side * grid_side))(device_keys)
    places = places[:, :CAP].reshape(N_GROUP, N_LOCAL, CAP).astype(jnp.int32)
    slot_ids = jnp.arange(CAP, dtype=jnp.int32)
    live_slots = slot_ids[None, None, :] < live_count[:, :, None]
    places = jnp.where(live_slots, places, -1)
    local_ids = jnp.arange(N_LOCAL, dtype=jnp.int32).reshape(1, N_LOCAL, 1)
    entries = []
    for step_x in (-1, 0, 1):
        beside = jnp.roll(places, -step_x, axis=1)
        device_ok = (local_ids + step_x >= 0) & (local_ids + step_x < N_LOCAL)
        for step_y in (-1, 0, 1):
            for step_z in (-1, 0, 1):
                along_y = places // grid_side + step_y
                along_z = places % grid_side + step_z
                inside = (along_y >= 0) & (along_y < grid_side) & (along_z >= 0) & (along_z < grid_side) & live_slots & device_ok
                target = along_y * grid_side + along_z
                matches = beside[:, :, None, :] == target[:, :, :, None]
                located = jnp.any(matches, axis=3) & inside
                chosen = jnp.sum(matches.astype(jnp.int32) * slot_ids, axis=3)
                entries.append(jnp.where(located, chosen, -1))
    neighbours = jnp.stack(entries, axis=3).reshape(BLOCKS, 27)
    offsets = jax.random.randint(key_offset, (N_GROUP, N_LOCAL, 1), 0, N_GROUP)
    group_ids = jnp.arange(N_GROUP, dtype=jnp.int32).reshape(N_GROUP, 1, 1)
    targets = (group_ids + offsets + slot_ids // 2) % N_GROUP * SEND_CAP + slot_ids % 2
    targets = jnp.where(live_slots, targets, -1).reshape(BLOCKS)
    return (neighbours.astype(jnp.int32), targets.astype(jnp.int32))


def draw_neighbours(key, part):
    return layout(key)[0]


def draw_coarse_dest(key, part):
    return layout(key)[1]


def block_levels(key, shape, shards, least, top_value):
    gain, own = 1.0, jax.random.fold_in(key, 6)
    for dim, parts in shards:
        draws = jnp.exp(jax.random.uniform(jax.random.fold_in(own, dim), (parts,), jnp.float32, least / len(shards), top_value / len(shards)))
        gain = gain * jnp.repeat(draws, shape[dim] // parts).reshape([-1 if axis == dim else 1 for axis in range(len(shape))])
    return gain


def centred(rng, dims, spread, most, cuts=(), kind=jnp.bfloat16):
    factor_of = block_levels(rng, dims, cuts, -0.22, 0.18) if cuts else 1.0
    array = jax.random.normal(rng, dims, jnp.float32) * spread * factor_of
    return jnp.minimum(jnp.maximum(array, -most), most).astype(kind)


def setup_inputs(seed: int = 0) -> dict:
    key_of = jax.random.split(jax.random.key(seed), 14)
    return {
        "features": centred(key_of[0], (BLOCKS, C, SIDE**3), 1.0, 6.0, ((0, 32),)),
        "neighbours": draw_neighbours(jax.random.fold_in(key_of[13], 71), 0),
        "coarse_dest": draw_coarse_dest(jax.random.fold_in(key_of[13], 71), 0),
        "weight_first": centred(key_of[3], (C, 27 * C), (27 * C) ** -0.5, 0.21875),
        "bias_first": centred(key_of[4], (C,), 0.5, 3.0, (), jnp.float32),
        "reduce_weight": centred(key_of[5], (CC, 8 * C), (8 * C) ** -0.5, 0.375),
        "reduce_bias": centred(key_of[6], (CC,), 0.5, 3.0, (), jnp.float32),
        "weight_coarse": centred(key_of[7], (CC, 27 * CC), (27 * CC) ** -0.5, 0.15625),
        "bias_coarse": centred(key_of[8], (CC,), 0.5, 3.0, (), jnp.float32),
        "weight_up": centred(key_of[9], (C, CC), CC ** -0.5, 0.75),
        "bias_up": centred(key_of[10], (C,), 0.5, 3.0, (), jnp.float32),
        "weight_last": centred(key_of[11], (C, 54 * C), (54 * C) ** -0.5, 0.15625),
        "bias_last": centred(key_of[12], (C,), 0.5, 3.0, (), jnp.float32),
    }


def assemble(extended, slot_table):
    count = extended.shape[0]
    cube_side = extended.shape[3]
    slot_index = jnp.maximum(slot_table, 0)
    present = slot_table >= 0
    across = {-1: (0, 1), 0: (1, cube_side + 1), 1: (cube_side + 1, cube_side + 2)}
    within = {-1: (cube_side - 1, cube_side), 0: (0, cube_side), 1: (0, 1)}
    slabs = []
    for step_x in (-1, 0, 1):
        strips = []
        for step_y in (-1, 0, 1):
            pieces = []
            for step_z in (-1, 0, 1):
                direction = (step_x + 1) * 9 + (step_y + 1) * 3 + step_z + 1
                window = extended[:, :, slice(*across[step_x]), slice(*within[step_y]), slice(*within[step_z])]
                window = jnp.take(window, slot_index[:, direction], axis=0)
                keep_here = present[:, direction].reshape(count, 1, 1, 1, 1)
                pieces.append(jnp.where(keep_here, window, jnp.zeros((), window.dtype)))
            strips.append(jnp.concatenate(pieces, axis=4))
        slabs.append(jnp.concatenate(strips, axis=3))
    return jnp.concatenate(slabs, axis=2)


def conv_block(cube, weight):
    channels = cube.shape[0]
    cube_side = cube.shape[1] - 2
    outputs = weight.shape[0]
    kernel = weight.reshape(outputs, 3, 3, 3, channels).transpose(0, 4, 1, 2, 3)
    result = lax.conv_general_dilated(cube[None], kernel, (1, 1, 1), "VALID", dimension_numbers=("NCDHW", "OIDHW", "NCDHW"), preferred_element_type=jnp.float32)
    return result.reshape(outputs, cube_side ** 3)


def fine_layer(extended, slot_table, occupied_mask, weight, bias_vec):
    count, channels, padded, plane = extended.shape
    cube_side = padded - 2
    cubes = assemble(extended.reshape(count, channels, padded, cube_side, cube_side), slot_table)
    preact = lax.map(lambda cube: conv_block(cube, weight), cubes)
    return (occupied_mask[:, None, None] * jax.nn.silu(preact + bias_vec[None, :, None])).astype(jnp.bfloat16)


def stride_reduce(leading_output, reduce_weight, reduce_bias, occupied_mask):
    count, channels, cells_all = leading_output.shape
    coarse_side = SIDE // 2
    grouped = leading_output.reshape(count, channels, coarse_side, 2, coarse_side, 2, coarse_side, 2)
    grouped = grouped.transpose(0, 3, 5, 7, 1, 2, 4, 6).reshape(count, 8 * channels, coarse_side ** 3)
    preact = lax.map(lambda stacked: jnp.dot(reduce_weight, stacked, preferred_element_type=jnp.float32), grouped)
    return (occupied_mask[:, None, None] * jax.nn.silu(preact + reduce_bias[None, :, None])).astype(jnp.bfloat16)


def coarse_tiles(extended, slot_table):
    count, channels, padded, plane = extended.shape
    coarse_side = padded - 2
    cubes = assemble(extended.reshape(count, channels, padded, coarse_side, coarse_side), slot_table)
    cube_cells = padded ** 3
    tile_width = (cube_cells + 127) // 128 * 128
    flattened = cubes.reshape(count, channels, cube_cells)
    return jnp.pad(flattened, ((0, 0), (0, 0), (0, tile_width - cube_cells)))


def coarse_conv(tile_rows, keep_mask, weight_coarse, bias_coarse):
    channels = tile_rows.shape[1]
    padded = SIDE // 2 + 2

    def convolve(tile_row):
        cube = tile_row[:, :padded ** 3].reshape(channels, padded, padded, padded)
        return conv_block(cube, weight_coarse)

    preact = lax.map(convolve, tile_rows)
    return (keep_mask[:, None, None] * jax.nn.silu(preact + bias_coarse[None, :, None])).astype(jnp.bfloat16)


def upsample(coarse_out, weight_up, bias_up, occupied_mask):
    count = coarse_out.shape[0]
    coarse_side = SIDE // 2
    projected = lax.map(lambda stacked: jnp.dot(weight_up, stacked, preferred_element_type=jnp.float32), coarse_out)
    projected = projected + bias_up[None, :, None]
    channels = projected.shape[1]
    cubes = projected.reshape(count, channels, coarse_side, 1, coarse_side, 1, coarse_side, 1)
    cubes = jnp.broadcast_to(cubes, (count, channels, coarse_side, 2, coarse_side, 2, coarse_side, 2))
    return (occupied_mask[:, None, None] * cubes.reshape(count, channels, SIDE ** 3)).astype(jnp.bfloat16)


def faces_ref(values, cube_side):
    devices, count, channels, cells_all = values.shape
    device_grid = values.reshape(N_GROUP, N_LOCAL, count, channels, cube_side, cube_side * cube_side)
    zero_plane = jnp.zeros_like(device_grid[:, :1, :, :, :1, :])
    lower_plane = jnp.concatenate([zero_plane, device_grid[:, :-1, :, :, -1:, :]], axis=1)
    upper_plane = jnp.concatenate([device_grid[:, 1:, :, :, :1, :], zero_plane], axis=1)
    extended = jnp.concatenate([lower_plane, device_grid, upper_plane], axis=4)
    return extended.reshape(devices, count, channels, cube_side + 2, cube_side * cube_side)


def reference(features, neighbours, coarse_dest, weight_first, bias_first, reduce_weight, reduce_bias, weight_coarse, bias_coarse, weight_up, bias_up, weight_last, bias_last):
    devices = N_GROUP * N_LOCAL
    slot_table = neighbours.reshape(devices, CAP, 27).astype(jnp.int32)
    occupied_mask = (slot_table[:, :, 13] >= 0).astype(jnp.float32)
    targets = coarse_dest.reshape(devices, CAP).astype(jnp.int32)
    valid_mask = occupied_mask * (targets >= 0).astype(jnp.float32)
    fine_in = features.reshape(devices, CAP, C, SIDE ** 3)
    leading_output = lax.map(lambda input_grids: fine_layer(input_grids[0], input_grids[1], input_grids[2], weight_first, bias_first), (faces_ref(fine_in, SIDE), slot_table, occupied_mask))
    coarse_input = lax.map(lambda input_grids: stride_reduce(input_grids[0], reduce_weight, reduce_bias, input_grids[1]), (leading_output, occupied_mask))
    tile_rows = lax.map(lambda input_grids: coarse_tiles(input_grids[0], input_grids[1]), (faces_ref(coarse_input, SIDE // 2), slot_table))
    coarse_out = lax.map(lambda input_grids: coarse_conv(input_grids[0], input_grids[1], weight_coarse, bias_coarse), (tile_rows, valid_mask))
    group_ids = jnp.arange(N_GROUP, dtype=jnp.int32).reshape(N_GROUP, 1, 1)
    local_ids = jnp.arange(N_LOCAL, dtype=jnp.int32).reshape(1, N_LOCAL, 1)
    grid_targets = targets.reshape(N_GROUP, N_LOCAL, CAP)
    position = ((grid_targets // SEND_CAP * N_LOCAL + local_ids) * N_GROUP + group_ids) * SEND_CAP + grid_targets % SEND_CAP
    position = jnp.where(valid_mask.reshape(N_GROUP, N_LOCAL, CAP) > 0, position, BAL_SLOTS).reshape(-1).astype(jnp.int32)
    coarse_cells = (SIDE // 2) ** 3
    balanced_coarse = jnp.zeros((BAL_SLOTS, CC, coarse_cells), coarse_out.dtype)
    balanced_coarse = balanced_coarse.at[position].set(coarse_out.reshape(-1, CC, coarse_cells), mode="drop")
    upward = lax.map(lambda input_grids: upsample(input_grids[0], weight_up, bias_up, input_grids[1]), (coarse_out, occupied_mask))
    joined = jnp.concatenate([leading_output, upward], axis=2)
    decoded = lax.map(lambda input_grids: fine_layer(input_grids[0], input_grids[1], input_grids[2], weight_last, bias_last), (faces_ref(joined, SIDE), slot_table, occupied_mask))
    return decoded.reshape(BLOCKS, C, SIDE ** 3), balanced_coarse
```

```python
import functools

import jax
import jax.numpy as jnp
from jax import lax
from jax.experimental import pallas as pl
from jax.experimental.pallas import tpu as pltpu
from jax.sharding import PartitionSpec as P

SEND_CAP = 2
MESH = pl.DeviceIdType.MESH
F32 = jnp.float32
BF16 = jnp.bfloat16
I32 = jnp.int32


def iota(shape, dim):
    return lax.broadcasted_iota(I32, shape, dim)


def onehot(mask):
    return jnp.where(mask, 1.0, 0.0).astype(BF16)


def column(row):
    n = row.shape[1]
    wide = jnp.broadcast_to(row, (n, n))
    return jnp.sum(jnp.where(iota((n, n), 0) == iota((n, n), 1), wide, 0.0), axis=1, keepdims=True)


def silu(u):
    return u / (1.0 + jnp.exp(-u))


def shifted(v, s):
    if s == 0:
        return v
    return jnp.concatenate([v[:, s:], v[:, :s]], axis=1)


def dot(a, b):
    return jnp.dot(a, b, preferred_element_type=F32)


def kernel(
    sizes,
    nb,
    dest,
    x_ref,
    w1_ref,
    b1_ref,
    wr_ref,
    br_ref,
    wc_ref,
    bc_ref,
    wu_ref,
    bu_ref,
    w2_ref,
    b2_ref,
    out_ref,
    bal_ref,
    sx,
    rx,
    sc,
    rc,
    sf,
    rf,
    su,
    ru,
    sb,
    rb,
    t1,
    t2,
    tred,
    tc,
    tup,
    tout,
    tbal,
    w1,
    wc,
    w2f,
    w2u,
    lhs,
    pad,
    y1,
    y2,
    fst,
    cin,
    up,
    red,
    send_sem,
    recv_sem,
    bal_send,
    bal_recv,
):
    side, count, ch, cc, n_local, n_group = sizes
    half = side // 2
    face = side * side
    planes = side + 2
    me = lax.axis_index("local")
    grp = lax.axis_index("group")
    right, left = lax.rem(me + 1, n_local), lax.rem(me + n_local - 1, n_local)
    ends = (left, right)

    def exchange(e, src, dst):
        copies = []
        for d in (0, 1):
            copies.append(
                pltpu.make_async_remote_copy(
                    src_ref=src.at[d],
                    dst_ref=dst.at[d],
                    send_sem=send_sem.at[e, d],
                    recv_sem=recv_sem.at[e, d],
                    device_id={"local": ends[d]},
                    device_id_type=MESH,
                )
            )
        return copies

    barrier = pltpu.get_barrier_semaphore()
    for e in ends:
        pl.semaphore_signal(barrier, inc=1, device_id={"local": e}, device_id_type=MESH)
    for d in range(1, n_group):
        pl.semaphore_signal(
            barrier, inc=1, device_id={"group": lax.rem(grp + d, n_group)}, device_id_type=MESH
        )
    for t in range(count):
        sx[0, t] = x_ref[t, :, 0:face]
        sx[1, t] = x_ref[t, :, (side - 1) * face : side * face]
    pl.semaphore_wait(barrier, 2 + n_group - 1)
    ex = exchange(0, sx, rx)
    for c in ex:
        c.start()

    n = iota((1, 256), 1)
    ny, nz = n >> 4, n & 15
    py = jnp.where(ny == 0, side - 1, jnp.where(ny == side + 1, 0, ny - 1))
    pz = jnp.where(nz == 0, side - 1, jnp.where(nz == side + 1, 0, nz - 1))
    inside = (ny < planes) & (nz < planes)
    t1[...] = onehot(iota((face, 256), 0) == jnp.where(inside, py * side + pz, -1))
    t2[...] = onehot(iota((256, 256), 0) == jnp.where(inside, py * 16 + pz, -1))
    n2 = iota((1, 512), 1)
    uy, uz = (n2 >> 4) & 15, n2 & 15
    qy = jnp.where(uy == 0, side - 1, jnp.where(uy == side + 1, 0, uy - 1))
    qz = jnp.where(uz == 0, side - 1, jnp.where(uz == side + 1, 0, uz - 1))
    target = (n2 >> 8) * 64 + (qy >> 1) * 8 + (qz >> 1)
    target = jnp.where((uy < planes) & (uz < planes), target, -1)
    tup[...] = onehot(iota((128, 512), 0) == target)
    ry, rz = (n2 >> 3) & 7, n2 & 7
    target = ((n2 >> 6) & 1) * 256 + (2 * ry + ((n2 >> 8) & 1)) * 16 + 2 * rz + ((n2 >> 7) & 1)
    target = jnp.where((ry < half) & (rz < half), target, -1)
    tred[...] = onehot(iota((512, 512), 0) == target)
    n1 = iota((1, 128), 1)
    cy, cz = (n1 >> 3) & 7, n1 & 7
    sy = jnp.where(cy == 0, half - 1, jnp.where(cy == half + 1, 0, cy - 1))
    sz = jnp.where(cz == 0, half - 1, jnp.where(cz == half + 1, 0, cz - 1))
    target = (n1 >> 6) * 64 + sy * 8 + sz
    tc[...] = onehot(iota((128, 128), 0) == target)
    k = iota((256, 1), 0)
    ky, kz = k >> 4, k & 15
    target = jnp.where((ky < side) & (kz < side), ky * side + kz, -1)
    tout[...] = onehot(iota((256, face), 1) == target)
    k = iota((64 * half, 1), 0)
    kx, ky, kz = k >> 6, (k >> 3) & 7, k & 7
    target = jnp.where((ky < half) & (kz < half), (kx * half + ky) * half + kz, -1)
    tbal[...] = onehot(iota((64 * half, half**3), 1) == target)

    for p in range(3):
        w1[p * ch : (p + 1) * ch] = w1_ref[:, p * 9 * ch : (p + 1) * 9 * ch]
        wc[p * cc : (p + 1) * cc] = wc_ref[:, p * 9 * cc : (p + 1) * 9 * cc]
        for part, dst in ((0, w2f), (1, w2u)):
            dst[p * ch : (p + 1) * ch] = jnp.concatenate(
                [
                    w2_ref[:, ((9 * p + k) * 2 + part) * ch : ((9 * p + k) * 2 + part + 1) * ch]
                    for k in range(9)
                ],
                axis=1,
            )
    b1, br, bc = column(b1_ref[...]), column(br_ref[...]), column(bc_ref[...])
    bu, b2 = column(bu_ref[...]), column(b2_ref[...])

    live = [jnp.where(nb[b, 13] >= 0, 1.0, 0.0) for b in range(count)]
    valid = [jnp.where(dest[b] >= 0, live[b], 0.0) for b in range(count)]

    def slot_row(b, step, dy, dz):
        row = jnp.zeros_like(dy)
        for iy in (-1, 0, 1):
            for iz in (-1, 0, 1):
                entry = nb[b, (step + 1) * 9 + (iy + 1) * 3 + iz + 1]
                row = jnp.where((dy == iy) & (dz == iz), entry, row)
        return row

    def as_masks(row):
        return [jnp.where(row == t, 1.0, 0.0) for t in range(count)]

    def offset(v, top):
        return jnp.where(v == 0, -1, jnp.where(v == top, 1, 0))

    fy, fz = offset(ny, side + 1), offset(nz, side + 1)
    gy, gz = offset(cy, half + 1), offset(cz, half + 1)
    fine = [[as_masks(slot_row(b, s, fy, fz)) for s in (-1, 0, 1)] for b in range(count)]
    mid = [as_masks(slot_row(b, 0, gy, gz)) for b in range(count)]
    rim = [
        as_masks(jnp.where(n1 < 64, slot_row(b, 1, gy, gz), slot_row(b, -1, gy, gz)))
        for b in range(count)
    ]

    def blend(parts, masks):
        total = parts[0] * masks[0]
        for part, mask in zip(parts[1:], masks[1:]):
            total = total + part * mask
        return total.astype(BF16)

    def taps(v, stride):
        return jnp.concatenate([shifted(v, q * stride + r) for q in range(3) for r in range(3)], axis=0)

    for t in range(count):
        for x in range(side):
            lhs[(x * count + t) * ch : (x * count + t + 1) * ch, 0:face] = x_ref[
                t, :, x * face : (x + 1) * face
            ]
    for x in range(side):
        a = dot(lhs[x * count * ch : (x + 1) * count * ch, 0:face], t1[...])
        parts = [a[t * ch : (t + 1) * ch] for t in range(count)]
        for b in range(count):
            rows = taps(blend(parts, fine[b][1]), 16)
            y1[b, x + 1] = dot(w1[...], rows)
    for c in ex:
        c.wait()
    for d, plane, step in ((1, 0, 0), (0, side + 1, 2)):
        a = dot(jnp.concatenate([rx[d, t] for t in range(count)], axis=0), t1[...])
        parts = [a[t * ch : (t + 1) * ch] for t in range(count)]
        for b in range(count):
            rows = taps(blend(parts, fine[b][step]), 16)
            y1[b, plane] = dot(w1[...], rows)
    for b in range(count):
        for x in range(side):
            u = y1[b, x, 0:ch] + y1[b, x + 1, ch : 2 * ch] + y1[b, x + 2, 2 * ch : 3 * ch] + b1
            fst[b, x] = (live[b] * silu(u)).astype(BF16)

    for b in range(count):
        sf[0, b] = fst[b, 0]
        sf[1, b] = fst[b, side - 1]
    pairs = half // 2
    for b in range(count):
        for j in range(pairs):
            for p in (0, 1):
                r0 = ((b * pairs + j) * 2 + p) * ch
                lhs[r0 : r0 + ch, 0:256] = fst[b, 4 * j + p]
                lhs[r0 : r0 + ch, 256:512] = fst[b, 4 * j + 2 + p]
    red[...] = dot(lhs[0 : count * pairs * 2 * ch, :], tred[...]).astype(BF16)
    for b in range(count):
        for j in range(pairs):
            r0 = (b * pairs + j) * 2 * ch
            rows = jnp.concatenate(
                [
                    red[r0 + p * ch : r0 + (p + 1) * ch, k * 128 : (k + 1) * 128]
                    for p in (0, 1)
                    for k in range(4)
                ],
                axis=0,
            )
            v = (live[b] * silu(dot(wr_ref[...], rows) + br)).astype(BF16)
            cin[b, j] = v
            if j == 0:
                sc[0, b] = v
            if j == pairs - 1:
                sc[1, b] = v
    ec, ef = exchange(1, sc, rc), exchange(2, sf, rf)
    for c in ec + ef:
        c.start()

    for x in range(side):
        a = dot(jnp.concatenate([fst[t, x] for t in range(count)], axis=0), t2[...])
        parts = [a[t * ch : (t + 1) * ch] for t in range(count)]
        for b in range(count):
            y1[b, x + 1] = dot(w2f[...], taps(blend(parts, fine[b][1]), 16))

    for j in range(pairs):
        a = dot(jnp.concatenate([cin[t, j] for t in range(count)], axis=0), tc[...])
        parts = [a[t * cc : (t + 1) * cc] for t in range(count)]
        for b in range(count):
            pad[b, j] = blend(parts, mid[b])
    for c in ec:
        c.wait()
    edge = [jnp.where(n1 < 64, rc[0, t].astype(F32), rc[1, t].astype(F32)).astype(BF16) for t in range(count)]
    a = dot(jnp.concatenate(edge, axis=0), tc[...])
    parts = [a[t * cc : (t + 1) * cc] for t in range(count)]
    for b in range(count):
        pad[b, pairs] = blend(parts, rim[b])
    coarse = []
    for b in range(count):
        ys = []
        for j in range(pairs + 1):
            ys.append(dot(wc[...], taps(pad[b, j], 8)))
        y = jnp.concatenate(ys, axis=1)
        width = y.shape[1]
        u = pltpu.roll(y[0:cc], 64, 1) + y[cc : 2 * cc] + pltpu.roll(y[2 * cc :], width - 64, 1) + bc
        co = (valid[b] * silu(u[:, 0 : 64 * half])).astype(BF16)
        coarse.append(co)
        v = (live[b] * (dot(wu_ref[...], co) + bu)).astype(BF16)
        for j in range(pairs):
            up[b, j] = v[:, j * 128 : (j + 1) * 128]
        su[0, b] = v[:, 0:128]
        su[1, b] = v[:, (pairs - 1) * 128 : pairs * 128]
    eu = exchange(3, su, ru)
    for c in eu:
        c.start()

    dense = [dot(co, tbal[...]) for co in coarse]

    def outgoing(r, k):
        total = jnp.zeros_like(dense[0])
        for b in range(count):
            total = total + dense[b] * jnp.where(dest[b] == r * SEND_CAP + k, valid[b], 0.0)
        return total.astype(BF16)

    sent = []
    for d in range(1, n_group):
        other = lax.rem(grp + d, n_group)
        for k in range(SEND_CAP):
            sb[d - 1, k] = outgoing(other, k)
        c = pltpu.make_async_remote_copy(
            src_ref=sb.at[d - 1],
            dst_ref=rb.at[d - 1],
            send_sem=bal_send.at[d - 1],
            recv_sem=bal_recv.at[d - 1],
            device_id={"group": other},
            device_id_type=MESH,
        )
        c.start()
        sent.append(c)
    for k in range(SEND_CAP):
        bal_ref[grp * SEND_CAP + k] = outgoing(grp, k)

    for c in ef:
        c.wait()
    for d, plane, step in ((1, 0, 0), (0, side + 1, 2)):
        a = dot(jnp.concatenate([rf[d, t] for t in range(count)], axis=0), t2[...])
        parts = [a[t * ch : (t + 1) * ch] for t in range(count)]
        for b in range(count):
            y1[b, plane] = dot(w2f[...], taps(blend(parts, fine[b][step]), 16))

    for j in range(pairs):
        a = dot(jnp.concatenate([up[t, j] for t in range(count)], axis=0), tup[...])
        for h in (0, 1):
            parts = [a[t * ch : (t + 1) * ch, h * 256 : (h + 1) * 256] for t in range(count)]
            for b in range(count):
                y2[b, 1 + 2 * j + h] = dot(w2u[...], taps(blend(parts, fine[b][1]), 16))
    for c in eu:
        c.wait()
    for d, plane, step, h in ((1, 0, 0, 1), (0, half + 1, 2, 0)):
        a = dot(jnp.concatenate([ru[d, t] for t in range(count)], axis=0), tup[:, h * 256 : (h + 1) * 256])
        parts = [a[t * ch : (t + 1) * ch] for t in range(count)]
        for b in range(count):
            y2[b, plane] = dot(w2u[...], taps(blend(parts, fine[b][step]), 16))

    for b in range(count):
        done = []
        for x in range(side):
            u = b2
            for p in range(3):
                u = u + y1[b, x + p, p * ch : (p + 1) * ch]
                u = u + y2[b, (x + p + 1) // 2, p * ch : (p + 1) * ch]
            lhs[x * ch : (x + 1) * ch, 0:256] = (live[b] * silu(u)).astype(BF16)
        flat = dot(lhs[0 : side * ch, 0:256], tout[...])
        for x in range(side):
            out_ref[b, :, x * face : (x + 1) * face] = flat[x * ch : (x + 1) * ch].astype(BF16)

    for d, c in enumerate(sent):
        c.wait()
        source = lax.rem(grp + n_group - (d + 1), n_group)
        for k in range(SEND_CAP):
            bal_ref[source * SEND_CAP + k] = rb[d, k]


def local(n_local, n_group, features, neighbours, coarse_dest, *weights):
    count, ch, cells = features.shape
    side = round(cells ** (1 / 3))
    cc = weights[2].shape[0]
    half, face = side // 2, side * side
    pairs = half // 2
    if side + 2 > 16 or half + 2 > 8 or half % 2 or side**3 != cells:
        raise ValueError("side")
    vmem = lambda *shape: pltpu.VMEM(shape, BF16)
    weights = [w.reshape(1, -1) if w.ndim == 1 else w for w in weights]
    whole = pl.BlockSpec(memory_space=pltpu.VMEM)
    smem = pl.BlockSpec(memory_space=pltpu.SMEM)
    return pl.pallas_call(
        functools.partial(kernel, (side, count, ch, cc, n_local, n_group)),
        out_shape=(
            jax.ShapeDtypeStruct(features.shape, BF16),
            jax.ShapeDtypeStruct((n_group * SEND_CAP, cc, half**3), BF16),
        ),
        in_specs=[smem, smem] + [whole] * (1 + len(weights)),
        out_specs=(whole, whole),
        scratch_shapes=[
            vmem(2, count, ch, face),
            vmem(2, count, ch, face),
            vmem(2, count, cc, 128),
            vmem(2, count, cc, 128),
            vmem(2, count, ch, 256),
            vmem(2, count, ch, 256),
            vmem(2, count, ch, 128),
            vmem(2, count, ch, 128),
            vmem(n_group - 1, SEND_CAP, cc, half**3),
            vmem(n_group - 1, SEND_CAP, cc, half**3),
            vmem(face, 256),
            vmem(256, 256),
            vmem(512, 512),
            vmem(128, 128),
            vmem(128, 512),
            vmem(256, face),
            vmem(64 * half, half**3),
            vmem(3 * ch, 9 * ch),
            vmem(3 * cc, 9 * cc),
            vmem(3 * ch, 9 * ch),
            vmem(3 * ch, 9 * ch),
            vmem(side * count * ch, 512),
            vmem(count, pairs + 1, cc, 128),
            pltpu.VMEM((count, side + 2, 3 * ch, 256), F32),
            pltpu.VMEM((count, half + 2, 3 * ch, 256), F32),
            vmem(count, side, ch, 256),
            vmem(count, pairs, cc, 128),
            vmem(count, pairs, ch, 128),
            vmem(count * pairs * 2 * ch, 512),
            pltpu.SemaphoreType.DMA((4, 2)),
            pltpu.SemaphoreType.DMA((4, 2)),
            pltpu.SemaphoreType.DMA((n_group - 1,)),
            pltpu.SemaphoreType.DMA((n_group - 1,)),
        ],
        compiler_params=pltpu.CompilerParams(collective_id=0, has_side_effects=True),
    )(neighbours, coarse_dest, features, *weights)


def solution(mesh):
    slots = P(("group", "local"), None, None)
    return jax.shard_map(
        functools.partial(local, mesh.shape["local"], mesh.shape["group"]),
        mesh=mesh,
        in_specs=(slots, P(("group", "local"), None), P(("group", "local"))) + (P(),) * 10,
        out_specs=(slots, slots),
        check_vma=False,
    )
```

```python
import functools

import jax
import jax.numpy as jnp
from jax import lax
from jax.experimental import pallas as pl
from jax.experimental.pallas import tpu as pltpu
from jax.sharding import PartitionSpec as P

SEND_CAP = 2
MESH = pl.DeviceIdType.MESH
F32 = jnp.float32
BF16 = jnp.bfloat16
I32 = jnp.int32


def iota(shape, dim):
    return lax.broadcasted_iota(I32, shape, dim)


def onehot(mask):
    return jnp.where(mask, 1.0, 0.0).astype(BF16)


def column(row):
    n = row.shape[1]
    wide = jnp.broadcast_to(row, (n, n))
    return jnp.sum(jnp.where(iota((n, n), 0) == iota((n, n), 1), wide, 0.0), axis=1, keepdims=True)


def silu(u):
    return u / (1.0 + jnp.exp(-u))


def shifted(v, s):
    if s == 0:
        return v
    return jnp.concatenate([v[:, s:], v[:, :s]], axis=1)


def dot(a, b):
    return jnp.dot(a, b, preferred_element_type=F32)


def kernel(
    sizes,
    nb,
    dest,
    x_ref,
    w1_ref,
    b1_ref,
    wr_ref,
    br_ref,
    wc_ref,
    bc_ref,
    wu_ref,
    bu_ref,
    w2_ref,
    b2_ref,
    out_ref,
    bal_ref,
    sx,
    rx,
    sc,
    rc,
    sf,
    rf,
    su,
    ru,
    sb,
    rb,
    t1,
    t2,
    tred,
    tc,
    tup,
    tout,
    tbal,
    w1,
    wc,
    w2f,
    w2u,
    lhs,
    pad,
    y1,
    y2,
    fst,
    cin,
    up,
    red,
    sel,
    fm,
    cm,
    send_sem,
    recv_sem,
    bal_send,
    bal_recv,
):
    side, count, ch, cc, n_local, n_group = sizes
    half = side // 2
    face = side * side
    planes = side + 2
    me = lax.axis_index("local")
    grp = lax.axis_index("group")
    right, left = lax.rem(me + 1, n_local), lax.rem(me + n_local - 1, n_local)
    ends = (left, right)
    has_left, has_right = me > 0, me < n_local - 1
    sends, receives = (has_left, has_right), (has_right, has_left)

    def exchange(e, src, dst):
        copies = []
        for d in (0, 1):
            copies.append(
                pltpu.make_async_remote_copy(
                    src_ref=src.at[d],
                    dst_ref=dst.at[d],
                    send_sem=send_sem.at[e, d],
                    recv_sem=recv_sem.at[e, d],
                    device_id={"local": ends[d]},
                    device_id_type=MESH,
                )
            )
        return copies

    def start(copies):
        for d in (0, 1):
            pl.when(sends[d])(copies[d].start)

    def receive(copies):
        for d in (0, 1):
            pl.when(receives[d])(copies[d].wait_recv)

    def finish(copies):
        for d in (0, 1):
            pl.when(sends[d])(copies[d].wait_send)

    for d in (0, 1):

        @pl.when(jnp.logical_not(receives[d]))
        def _():
            for buf in (rx, rc, rf, ru):
                buf[d] = jnp.zeros(buf.shape[1:], BF16)

    barrier = pltpu.get_barrier_semaphore()
    for d in (0, 1):

        @pl.when(sends[d])
        def _():
            pl.semaphore_signal(barrier, inc=1, device_id={"local": ends[d]}, device_id_type=MESH)

    for d in range(1, n_group):
        pl.semaphore_signal(
            barrier, inc=1, device_id={"group": lax.rem(grp + d, n_group)}, device_id_type=MESH
        )
    for t in range(count):
        sx[0, t] = x_ref[t, :, 0:face]
        sx[1, t] = x_ref[t, :, (side - 1) * face : side * face]
    n = iota((1, 256), 1)
    ny, nz = n >> 4, n & 15
    py = jnp.where(ny == 0, side - 1, jnp.where(ny == side + 1, 0, ny - 1))
    pz = jnp.where(nz == 0, side - 1, jnp.where(nz == side + 1, 0, nz - 1))
    inside = (ny < planes) & (nz < planes)
    t1[...] = onehot(iota((face, 256), 0) == jnp.where(inside, py * side + pz, -1))
    t2[...] = onehot(iota((256, 256), 0) == jnp.where(inside, py * 16 + pz, -1))
    n2 = iota((1, 512), 1)
    uy, uz = (n2 >> 4) & 15, n2 & 15
    qy = jnp.where(uy == 0, side - 1, jnp.where(uy == side + 1, 0, uy - 1))
    qz = jnp.where(uz == 0, side - 1, jnp.where(uz == side + 1, 0, uz - 1))
    target = (n2 >> 8) * 64 + (qy >> 1) * 8 + (qz >> 1)
    target = jnp.where((uy < planes) & (uz < planes), target, -1)
    tup[...] = onehot(iota((128, 512), 0) == target)
    ry, rz = (n2 >> 3) & 7, n2 & 7
    target = ((n2 >> 6) & 1) * 256 + (2 * ry + ((n2 >> 8) & 1)) * 16 + 2 * rz + ((n2 >> 7) & 1)
    target = jnp.where((ry < half) & (rz < half), target, -1)
    tred[...] = onehot(iota((512, 512), 0) == target)
    n1 = iota((1, 128), 1)
    cy, cz = (n1 >> 3) & 7, n1 & 7
    sy = jnp.where(cy == 0, half - 1, jnp.where(cy == half + 1, 0, cy - 1))
    sz = jnp.where(cz == 0, half - 1, jnp.where(cz == half + 1, 0, cz - 1))
    target = (n1 >> 6) * 64 + sy * 8 + sz
    tc[...] = onehot(iota((128, 128), 0) == target)
    k = iota((256, 1), 0)
    ky, kz = k >> 4, k & 15
    target = jnp.where((ky < side) & (kz < side), ky * side + kz, -1)
    tout[...] = onehot(iota((256, face), 1) == target)
    k = iota((64 * half, 1), 0)
    kx, ky, kz = k >> 6, (k >> 3) & 7, k & 7
    target = jnp.where((ky < half) & (kz < half), (kx * half + ky) * half + kz, -1)
    tbal[...] = onehot(iota((64 * half, half**3), 1) == target)

    for p in range(3):
        w1[p * ch : (p + 1) * ch] = w1_ref[:, p * 9 * ch : (p + 1) * 9 * ch]
        wc[p * cc : (p + 1) * cc] = wc_ref[:, p * 9 * cc : (p + 1) * 9 * cc]
        for part, dst in ((0, w2f), (1, w2u)):
            dst[p * ch : (p + 1) * ch] = jnp.concatenate(
                [
                    w2_ref[:, ((9 * p + k) * 2 + part) * ch : ((9 * p + k) * 2 + part + 1) * ch]
                    for k in range(9)
                ],
                axis=1,
            )
    b1, br, bc = column(b1_ref[...]), column(br_ref[...]), column(bc_ref[...])
    bu, b2 = column(bu_ref[...]), column(b2_ref[...])

    live = [jnp.where(nb[b, 13] >= 0, 1.0, 0.0) for b in range(count)]
    valid = [jnp.where(dest[b] >= 0, live[b], 0.0) for b in range(count)]

    def slot_row(b, step, dy, dz):
        row = jnp.zeros_like(dy)
        for iy in (-1, 0, 1):
            for iz in (-1, 0, 1):
                entry = nb[b, (step + 1) * 9 + (iy + 1) * 3 + iz + 1]
                row = jnp.where((dy == iy) & (dz == iz), entry, row)
        return row

    def as_masks(row):
        return [jnp.where(row == t, 1.0, 0.0) for t in range(count)]

    def offset(v, top):
        return jnp.where(v == 0, -1, jnp.where(v == top, 1, 0))

    fy, fz = offset(ny, side + 1), offset(nz, side + 1)
    gy, gz = offset(cy, half + 1), offset(cz, half + 1)
    fine = [[as_masks(slot_row(b, s, fy, fz)) for s in (-1, 0, 1)] for b in range(count)]
    mid = [as_masks(slot_row(b, 0, gy, gz)) for b in range(count)]
    rim = [
        as_masks(jnp.where(n1 < 64, slot_row(b, 1, gy, gz), slot_row(b, -1, gy, gz)))
        for b in range(count)
    ]

    for b in range(count):
        for t in range(count):
            for s in range(3):
                fm[b, s, t] = jnp.broadcast_to(fine[b][s][t], (ch, 256)).astype(BF16)
            cm[b, 0, t] = jnp.broadcast_to(mid[b][t], (cc, 128)).astype(BF16)
            cm[b, 1, t] = jnp.broadcast_to(rim[b][t], (cc, 128)).astype(BF16)

    def blend(parts, masks):
        total = parts[0] * masks[0]
        for t in range(1, count):
            total = total + parts[t] * masks[t]
        return total

    def taps(v, stride):
        return jnp.concatenate([shifted(v, q * stride + r) for q in range(3) for r in range(3)], axis=0)

    for t in range(count):
        for x in range(side):
            lhs[(x * count + t) * ch : (x * count + t + 1) * ch, 0:face] = x_ref[
                t, :, x * face : (x + 1) * face
            ]
    beside = jnp.where(has_left, 1, 0) + jnp.where(has_right, 1, 0)
    pl.semaphore_wait(barrier, beside + n_group - 1)
    ex = exchange(0, sx, rx)
    start(ex)
    sel[...] = dot(lhs[:, 0:face], t1[...]).astype(BF16)
    for x in range(side):
        parts = [sel[(x * count + t) * ch : (x * count + t + 1) * ch] for t in range(count)]
        for b in range(count):
            rows = taps(blend(parts, fm.at[b, 1]), 16)
            y1[b, x + 1] = dot(w1[...], rows)
    receive(ex)
    for d, plane, step in ((1, 0, 0), (0, side + 1, 2)):
        a = dot(jnp.concatenate([rx[d, t] for t in range(count)], axis=0), t1[...]).astype(BF16)
        parts = [a[t * ch : (t + 1) * ch] for t in range(count)]
        for b in range(count):
            rows = taps(blend(parts, fm.at[b, step]), 16)
            y1[b, plane] = dot(w1[...], rows)
    for b in range(count):
        for x in range(side):
            u = y1[b, x, 0:ch] + y1[b, x + 1, ch : 2 * ch] + y1[b, x + 2, 2 * ch : 3 * ch] + b1
            fst[b, x] = (live[b] * silu(u)).astype(BF16)

    for b in range(count):
        sf[0, b] = fst[b, 0]
        sf[1, b] = fst[b, side - 1]
    pairs = half // 2
    for b in range(count):
        for j in range(pairs):
            for p in (0, 1):
                r0 = ((b * pairs + j) * 2 + p) * ch
                lhs[r0 : r0 + ch, 0:256] = fst[b, 4 * j + p]
                lhs[r0 : r0 + ch, 256:512] = fst[b, 4 * j + 2 + p]
    red[...] = dot(lhs[0 : count * pairs * 2 * ch, :], tred[...]).astype(BF16)
    for b in range(count):
        for j in range(pairs):
            r0 = (b * pairs + j) * 2 * ch
            rows = jnp.concatenate(
                [
                    red[r0 + p * ch : r0 + (p + 1) * ch, k * 128 : (k + 1) * 128]
                    for p in (0, 1)
                    for k in range(4)
                ],
                axis=0,
            )
            v = (live[b] * silu(dot(wr_ref[...], rows) + br)).astype(BF16)
            cin[b, j] = v
            if j == 0:
                sc[0, b] = v
            if j == pairs - 1:
                sc[1, b] = v
    ec, ef = exchange(1, sc, rc), exchange(2, sf, rf)
    start(ec)
    start(ef)

    for t in range(count):
        for x in range(side):
            lhs[(x * count + t) * ch : (x * count + t + 1) * ch, 0:256] = fst[t, x]
    sel[...] = dot(lhs[:, 0:256], t2[...]).astype(BF16)
    for x in range(side):
        parts = [sel[(x * count + t) * ch : (x * count + t + 1) * ch] for t in range(count)]
        for b in range(count):
            y1[b, x + 1] = dot(w2f[...], taps(blend(parts, fm.at[b, 1]), 16))

    for j in range(pairs):
        a = dot(jnp.concatenate([cin[t, j] for t in range(count)], axis=0), tc[...]).astype(BF16)
        parts = [a[t * cc : (t + 1) * cc] for t in range(count)]
        for b in range(count):
            pad[b, j] = blend(parts, cm.at[b, 0])
    receive(ec)
    edge = [jnp.where(n1 < 64, rc[0, t].astype(F32), rc[1, t].astype(F32)).astype(BF16) for t in range(count)]
    a = dot(jnp.concatenate(edge, axis=0), tc[...]).astype(BF16)
    parts = [a[t * cc : (t + 1) * cc] for t in range(count)]
    for b in range(count):
        pad[b, pairs] = blend(parts, cm.at[b, 1])
    coarse = []
    for b in range(count):
        ys = []
        for j in range(pairs + 1):
            ys.append(dot(wc[...], taps(pad[b, j], 8)))
        y = jnp.concatenate(ys, axis=1)
        width = y.shape[1]
        u = pltpu.roll(y[0:cc], 64, 1) + y[cc : 2 * cc] + pltpu.roll(y[2 * cc :], width - 64, 1) + bc
        co = (valid[b] * silu(u[:, 0 : 64 * half])).astype(BF16)
        coarse.append(co)
        v = (live[b] * (dot(wu_ref[...], co) + bu)).astype(BF16)
        for j in range(pairs):
            up[b, j] = v[:, j * 128 : (j + 1) * 128]
        su[0, b] = v[:, 0:128]
        su[1, b] = v[:, (pairs - 1) * 128 : pairs * 128]
    eu = exchange(3, su, ru)
    start(eu)

    dense = [dot(co, tbal[...]) for co in coarse]

    def outgoing(r, k):
        total = jnp.zeros_like(dense[0])
        for b in range(count):
            total = total + dense[b] * jnp.where(dest[b] == r * SEND_CAP + k, valid[b], 0.0)
        return total.astype(BF16)

    sent = []
    for d in range(1, n_group):
        other = lax.rem(grp + d, n_group)
        for k in range(SEND_CAP):
            sb[d - 1, k] = outgoing(other, k)
        c = pltpu.make_async_remote_copy(
            src_ref=sb.at[d - 1],
            dst_ref=rb.at[d - 1],
            send_sem=bal_send.at[d - 1],
            recv_sem=bal_recv.at[d - 1],
            device_id={"group": other},
            device_id_type=MESH,
        )
        c.start()
        sent.append(c)
    for k in range(SEND_CAP):
        bal_ref[grp * SEND_CAP + k] = outgoing(grp, k)

    receive(ef)
    for d, plane, step in ((1, 0, 0), (0, side + 1, 2)):
        a = dot(jnp.concatenate([rf[d, t] for t in range(count)], axis=0), t2[...]).astype(BF16)
        parts = [a[t * ch : (t + 1) * ch] for t in range(count)]
        for b in range(count):
            y1[b, plane] = dot(w2f[...], taps(blend(parts, fm.at[b, step]), 16))

    for j in range(pairs):
        a = dot(jnp.concatenate([up[t, j] for t in range(count)], axis=0), tup[...]).astype(BF16)
        for h in (0, 1):
            parts = [a[t * ch : (t + 1) * ch, h * 256 : (h + 1) * 256] for t in range(count)]
            for b in range(count):
                y2[b, 1 + 2 * j + h] = dot(w2u[...], taps(blend(parts, fm.at[b, 1]), 16))
    receive(eu)
    for d, plane, step, h in ((1, 0, 0, 1), (0, half + 1, 2, 0)):
        a = dot(jnp.concatenate([ru[d, t] for t in range(count)], axis=0), tup[:, h * 256 : (h + 1) * 256]).astype(BF16)
        parts = [a[t * ch : (t + 1) * ch] for t in range(count)]
        for b in range(count):
            y2[b, plane] = dot(w2u[...], taps(blend(parts, fm.at[b, step]), 16))

    for b in range(count):
        done = []
        for x in range(side):
            u = b2
            for p in range(3):
                u = u + y1[b, x + p, p * ch : (p + 1) * ch]
                u = u + y2[b, (x + p + 1) // 2, p * ch : (p + 1) * ch]
            lhs[x * ch : (x + 1) * ch, 0:256] = (live[b] * silu(u)).astype(BF16)
        flat = dot(lhs[0 : side * ch, 0:256], tout[...])
        for x in range(side):
            out_ref[b, :, x * face : (x + 1) * face] = flat[x * ch : (x + 1) * ch].astype(BF16)

    for copies in (ex, ec, ef, eu):
        finish(copies)
    for d, c in enumerate(sent):
        c.wait()
        source = lax.rem(grp + n_group - (d + 1), n_group)
        for k in range(SEND_CAP):
            bal_ref[source * SEND_CAP + k] = rb[d, k]


def local(n_local, n_group, features, neighbours, coarse_dest, *weights):
    count, ch, cells = features.shape
    side = round(cells ** (1 / 3))
    cc = weights[2].shape[0]
    half, face = side // 2, side * side
    pairs = half // 2
    if side + 2 > 16 or half + 2 > 8 or half % 2 or side**3 != cells:
        raise ValueError("side")
    vmem = lambda *shape: pltpu.VMEM(shape, BF16)
    weights = [w.reshape(1, -1) if w.ndim == 1 else w for w in weights]
    whole = pl.BlockSpec(memory_space=pltpu.VMEM)
    smem = pl.BlockSpec(memory_space=pltpu.SMEM)
    return pl.pallas_call(
        functools.partial(kernel, (side, count, ch, cc, n_local, n_group)),
        out_shape=(
            jax.ShapeDtypeStruct(features.shape, BF16),
            jax.ShapeDtypeStruct((n_group * SEND_CAP, cc, half**3), BF16),
        ),
        in_specs=[smem, smem] + [whole] * (1 + len(weights)),
        out_specs=(whole, whole),
        scratch_shapes=[
            vmem(2, count, ch, face),
            vmem(2, count, ch, face),
            vmem(2, count, cc, 128),
            vmem(2, count, cc, 128),
            vmem(2, count, ch, 256),
            vmem(2, count, ch, 256),
            vmem(2, count, ch, 128),
            vmem(2, count, ch, 128),
            vmem(n_group - 1, SEND_CAP, cc, half**3),
            vmem(n_group - 1, SEND_CAP, cc, half**3),
            vmem(face, 256),
            vmem(256, 256),
            vmem(512, 512),
            vmem(128, 128),
            vmem(128, 512),
            vmem(256, face),
            vmem(64 * half, half**3),
            vmem(3 * ch, 9 * ch),
            vmem(3 * cc, 9 * cc),
            vmem(3 * ch, 9 * ch),
            vmem(3 * ch, 9 * ch),
            vmem(side * count * ch, 512),
            vmem(count, pairs + 1, cc, 128),
            pltpu.VMEM((count, side + 2, 3 * ch, 256), F32),
            pltpu.VMEM((count, half + 2, 3 * ch, 256), F32),
            vmem(count, side, ch, 256),
            vmem(count, pairs, cc, 128),
            vmem(count, pairs, ch, 128),
            vmem(count * pairs * 2 * ch, 512),
            vmem(side * count * ch, 256),
            vmem(count, 3, count, ch, 256),
            vmem(count, 2, count, cc, 128),
            pltpu.SemaphoreType.DMA((4, 2)),
            pltpu.SemaphoreType.DMA((4, 2)),
            pltpu.SemaphoreType.DMA((n_group - 1,)),
            pltpu.SemaphoreType.DMA((n_group - 1,)),
        ],
        compiler_params=pltpu.CompilerParams(collective_id=0, has_side_effects=True),
    )(neighbours, coarse_dest, features, *weights)


def solution(mesh):
    slots = P(("group", "local"), None, None)
    return jax.shard_map(
        functools.partial(local, mesh.shape["local"], mesh.shape["group"]),
        mesh=mesh,
        in_specs=(slots, P(("group", "local"), None), P(("group", "local"))) + (P(),) * 10,
        out_specs=(slots, slots),
        check_vma=False,
    )
```

```python
import functools

import jax
import jax.numpy as jnp
from jax import lax
from jax.experimental import pallas as pl
from jax.experimental.pallas import tpu as pltpu
from jax.sharding import PartitionSpec as P

SEND_CAP = 2
MESH = pl.DeviceIdType.MESH
F32 = jnp.float32
BF16 = jnp.bfloat16
I32 = jnp.int32


def iota(shape, dim):
    return lax.broadcasted_iota(I32, shape, dim)


def onehot(mask):
    return jnp.where(mask, 1.0, 0.0).astype(BF16)


def column(row):
    n = row.shape[1]
    wide = jnp.broadcast_to(row, (n, n))
    return jnp.sum(jnp.where(iota((n, n), 0) == iota((n, n), 1), wide, 0.0), axis=1, keepdims=True)


def silu(u):
    return u / (1.0 + jnp.exp(-u))


def shifted(v, s):
    if s == 0:
        return v
    return jnp.concatenate([v[:, s:], v[:, :s]], axis=1)


def dot(a, b):
    return jnp.dot(a, b, preferred_element_type=F32)


def kernel(
    sizes,
    nb,
    dest,
    x_ref,
    w1_ref,
    b1_ref,
    wr_ref,
    br_ref,
    wc_ref,
    bc_ref,
    wu_ref,
    bu_ref,
    w2_ref,
    b2_ref,
    out_ref,
    bal_ref,
    sx,
    rx,
    sc,
    rc,
    sf,
    rf,
    su,
    ru,
    sb,
    rb,
    t1,
    t2,
    tred,
    tc,
    tup,
    tout,
    tbal,
    w1,
    wc,
    w2f,
    w2u,
    lhs,
    pad,
    y1,
    y2,
    fst,
    cin,
    up,
    red,
    sel,
    fm,
    cm,
    send_sem,
    recv_sem,
    bal_send,
    bal_recv,
):
    side, count, ch, cc, n_local, n_group = sizes
    half = side // 2
    face = side * side
    planes = side + 2
    me = lax.axis_index("local")
    grp = lax.axis_index("group")
    right, left = lax.rem(me + 1, n_local), lax.rem(me + n_local - 1, n_local)
    ends = (left, right)
    has_left, has_right = me > 0, me < n_local - 1
    sends, receives = (has_left, has_right), (has_right, has_left)

    def exchange(e, src, dst):
        copies = []
        for d in (0, 1):
            copies.append(
                pltpu.make_async_remote_copy(
                    src_ref=src.at[d],
                    dst_ref=dst.at[d],
                    send_sem=send_sem.at[e, d],
                    recv_sem=recv_sem.at[e, d],
                    device_id={"local": ends[d]},
                    device_id_type=MESH,
                )
            )
        return copies

    def start(copies):
        for d in (0, 1):
            pl.when(sends[d])(copies[d].start)

    def receive(copies):
        for d in (0, 1):
            pl.when(receives[d])(copies[d].wait_recv)

    def finish(copies):
        for d in (0, 1):
            pl.when(sends[d])(copies[d].wait_send)

    for d in (0, 1):

        @pl.when(jnp.logical_not(receives[d]))
        def _():
            for buf in (rx, rc, rf, ru):
                buf[d] = jnp.zeros(buf.shape[1:], BF16)

    barrier = pltpu.get_barrier_semaphore()
    for d in (0, 1):

        @pl.when(sends[d])
        def _():
            pl.semaphore_signal(barrier, inc=1, device_id={"local": ends[d]}, device_id_type=MESH)

    for d in range(1, n_group):
        pl.semaphore_signal(
            barrier, inc=1, device_id={"group": lax.rem(grp + d, n_group)}, device_id_type=MESH
        )
    for t in range(count):
        sx[0, t] = x_ref[t, :, 0:face]
        sx[1, t] = x_ref[t, :, (side - 1) * face : side * face]
    n = iota((1, 256), 1)
    ny, nz = n >> 4, n & 15
    py = jnp.where(ny == 0, side - 1, jnp.where(ny == side + 1, 0, ny - 1))
    pz = jnp.where(nz == 0, side - 1, jnp.where(nz == side + 1, 0, nz - 1))
    inside = (ny < planes) & (nz < planes)
    t1[...] = onehot(iota((face, 256), 0) == jnp.where(inside, py * side + pz, -1))
    t2[...] = onehot(iota((256, 256), 0) == jnp.where(inside, py * 16 + pz, -1))
    n2 = iota((1, 512), 1)
    uy, uz = (n2 >> 4) & 15, n2 & 15
    qy = jnp.where(uy == 0, side - 1, jnp.where(uy == side + 1, 0, uy - 1))
    qz = jnp.where(uz == 0, side - 1, jnp.where(uz == side + 1, 0, uz - 1))
    target = (n2 >> 8) * 64 + (qy >> 1) * 8 + (qz >> 1)
    target = jnp.where((uy < planes) & (uz < planes), target, -1)
    tup[...] = onehot(iota((128, 512), 0) == target)
    ry, rz = (n2 >> 3) & 7, n2 & 7
    target = ((n2 >> 6) & 1) * 256 + (2 * ry + ((n2 >> 8) & 1)) * 16 + 2 * rz + ((n2 >> 7) & 1)
    target = jnp.where((ry < half) & (rz < half), target, -1)
    tred[...] = onehot(iota((512, 512), 0) == target)
    n1 = iota((1, 128), 1)
    cy, cz = (n1 >> 3) & 7, n1 & 7
    sy = jnp.where(cy == 0, half - 1, jnp.where(cy == half + 1, 0, cy - 1))
    sz = jnp.where(cz == 0, half - 1, jnp.where(cz == half + 1, 0, cz - 1))
    target = (n1 >> 6) * 64 + sy * 8 + sz
    tc[...] = onehot(iota((128, 128), 0) == target)
    k = iota((256, 1), 0)
    ky, kz = k >> 4, k & 15
    target = jnp.where((ky < side) & (kz < side), ky * side + kz, -1)
    tout[...] = onehot(iota((256, face), 1) == target)
    k = iota((64 * half, 1), 0)
    kx, ky, kz = k >> 6, (k >> 3) & 7, k & 7
    target = jnp.where((ky < half) & (kz < half), (kx * half + ky) * half + kz, -1)
    tbal[...] = onehot(iota((64 * half, half**3), 1) == target)

    for p in range(3):
        w1[p * ch : (p + 1) * ch] = w1_ref[:, p * 9 * ch : (p + 1) * 9 * ch]
        wc[p * cc : (p + 1) * cc] = wc_ref[:, p * 9 * cc : (p + 1) * 9 * cc]
        for part, dst in ((0, w2f), (1, w2u)):
            dst[p * ch : (p + 1) * ch] = jnp.concatenate(
                [
                    w2_ref[:, ((9 * p + k) * 2 + part) * ch : ((9 * p + k) * 2 + part + 1) * ch]
                    for k in range(9)
                ],
                axis=1,
            )
    b1, br, bc = column(b1_ref[...]), column(br_ref[...]), column(bc_ref[...])
    bu, b2 = column(bu_ref[...]), column(b2_ref[...])

    live = [jnp.where(nb[b, 13] >= 0, 1.0, 0.0) for b in range(count)]
    valid = [jnp.where(dest[b] >= 0, live[b], 0.0) for b in range(count)]

    def slot_row(b, step, dy, dz):
        row = jnp.zeros_like(dy)
        for iy in (-1, 0, 1):
            for iz in (-1, 0, 1):
                entry = nb[b, (step + 1) * 9 + (iy + 1) * 3 + iz + 1]
                row = jnp.where((dy == iy) & (dz == iz), entry, row)
        return row

    def as_masks(row):
        return [jnp.where(row == t, 1.0, 0.0) for t in range(count)]

    def offset(v, top):
        return jnp.where(v == 0, -1, jnp.where(v == top, 1, 0))

    fy, fz = offset(ny, side + 1), offset(nz, side + 1)
    gy, gz = offset(cy, half + 1), offset(cz, half + 1)
    fine = [[as_masks(slot_row(b, s, fy, fz)) for s in (-1, 0, 1)] for b in range(count)]
    mid = [as_masks(slot_row(b, 0, gy, gz)) for b in range(count)]
    rim = [
        as_masks(jnp.where(n1 < 64, slot_row(b, 1, gy, gz), slot_row(b, -1, gy, gz)))
        for b in range(count)
    ]

    for b in range(count):
        for t in range(count):
            for s in range(3):
                fm[b, s, t] = jnp.broadcast_to(fine[b][s][t], (ch, 256)).astype(BF16)
            cm[b, 0, t] = jnp.broadcast_to(mid[b][t], (cc, 128)).astype(BF16)
            cm[b, 1, t] = jnp.broadcast_to(rim[b][t], (cc, 128)).astype(BF16)

    def blend(parts, masks):
        total = parts[0] * masks[0]
        for t in range(1, count):
            total = total + parts[t] * masks[t]
        return total

    def taps(v, stride):
        return jnp.concatenate([shifted(v, q * stride + r) for q in range(3) for r in range(3)], axis=0)

    def convolve(dst, plane, weight, parts, step):
        both = [taps(blend(parts, fm.at[b, step]), 16) for b in range(count)]
        y = dot(weight[...], jnp.concatenate(both, axis=1))
        for b in range(count):
            dst[b, plane] = y[:, b * 256 : (b + 1) * 256]

    for t in range(count):
        for x in range(side):
            lhs[(x * count + t) * ch : (x * count + t + 1) * ch, 0:face] = x_ref[
                t, :, x * face : (x + 1) * face
            ]
    beside = jnp.where(has_left, 1, 0) + jnp.where(has_right, 1, 0)
    pl.semaphore_wait(barrier, beside + n_group - 1)
    ex = exchange(0, sx, rx)
    start(ex)
    sel[...] = dot(lhs[:, 0:face], t1[...]).astype(BF16)
    for x in range(side):
        parts = [sel[(x * count + t) * ch : (x * count + t + 1) * ch] for t in range(count)]
        convolve(y1, x + 1, w1, parts, 1)
    receive(ex)
    for d, plane, step in ((1, 0, 0), (0, side + 1, 2)):
        a = dot(jnp.concatenate([rx[d, t] for t in range(count)], axis=0), t1[...]).astype(BF16)
        parts = [a[t * ch : (t + 1) * ch] for t in range(count)]
        convolve(y1, plane, w1, parts, step)
    for b in range(count):
        for x in range(side):
            u = y1[b, x, 0:ch] + y1[b, x + 1, ch : 2 * ch] + y1[b, x + 2, 2 * ch : 3 * ch] + b1
            fst[b, x] = (live[b] * silu(u)).astype(BF16)

    for b in range(count):
        sf[0, b] = fst[b, 0]
        sf[1, b] = fst[b, side - 1]
    pairs = half // 2
    for b in range(count):
        for j in range(pairs):
            for p in (0, 1):
                r0 = ((b * pairs + j) * 2 + p) * ch
                lhs[r0 : r0 + ch, 0:256] = fst[b, 4 * j + p]
                lhs[r0 : r0 + ch, 256:512] = fst[b, 4 * j + 2 + p]
    red[...] = dot(lhs[0 : count * pairs * 2 * ch, :], tred[...]).astype(BF16)
    for b in range(count):
        for j in range(pairs):
            r0 = (b * pairs + j) * 2 * ch
            rows = jnp.concatenate(
                [
                    red[r0 + p * ch : r0 + (p + 1) * ch, k * 128 : (k + 1) * 128]
                    for p in (0, 1)
                    for k in range(4)
                ],
                axis=0,
            )
            v = (live[b] * silu(dot(wr_ref[...], rows) + br)).astype(BF16)
            cin[b, j] = v
            if j == 0:
                sc[0, b] = v
            if j == pairs - 1:
                sc[1, b] = v
    ec, ef = exchange(1, sc, rc), exchange(2, sf, rf)
    start(ec)
    start(ef)

    for t in range(count):
        for x in range(side):
            lhs[(x * count + t) * ch : (x * count + t + 1) * ch, 0:256] = fst[t, x]
    sel[...] = dot(lhs[:, 0:256], t2[...]).astype(BF16)
    for x in range(side):
        parts = [sel[(x * count + t) * ch : (x * count + t + 1) * ch] for t in range(count)]
        convolve(y1, x + 1, w2f, parts, 1)

    for j in range(pairs):
        a = dot(jnp.concatenate([cin[t, j] for t in range(count)], axis=0), tc[...]).astype(BF16)
        parts = [a[t * cc : (t + 1) * cc] for t in range(count)]
        for b in range(count):
            pad[b, j] = blend(parts, cm.at[b, 0])
    receive(ec)
    edge = [jnp.where(n1 < 64, rc[0, t].astype(F32), rc[1, t].astype(F32)).astype(BF16) for t in range(count)]
    a = dot(jnp.concatenate(edge, axis=0), tc[...]).astype(BF16)
    parts = [a[t * cc : (t + 1) * cc] for t in range(count)]
    for b in range(count):
        pad[b, pairs] = blend(parts, cm.at[b, 1])
    coarse = []
    for b in range(count):
        y = dot(wc[...], jnp.concatenate([taps(pad[b, j], 8) for j in range(pairs + 1)], axis=1))
        width = y.shape[1]
        u = pltpu.roll(y[0:cc], 64, 1) + y[cc : 2 * cc] + pltpu.roll(y[2 * cc :], width - 64, 1) + bc
        co = (valid[b] * silu(u[:, 0 : 64 * half])).astype(BF16)
        coarse.append(co)
        v = (live[b] * (dot(wu_ref[...], co) + bu)).astype(BF16)
        for j in range(pairs):
            up[b, j] = v[:, j * 128 : (j + 1) * 128]
        su[0, b] = v[:, 0:128]
        su[1, b] = v[:, (pairs - 1) * 128 : pairs * 128]
    eu = exchange(3, su, ru)
    start(eu)

    dense = [dot(co, tbal[...]) for co in coarse]

    def outgoing(r, k):
        total = jnp.zeros_like(dense[0])
        for b in range(count):
            total = total + dense[b] * jnp.where(dest[b] == r * SEND_CAP + k, valid[b], 0.0)
        return total.astype(BF16)

    sent = []
    for d in range(1, n_group):
        other = lax.rem(grp + d, n_group)
        for k in range(SEND_CAP):
            sb[d - 1, k] = outgoing(other, k)
        c = pltpu.make_async_remote_copy(
            src_ref=sb.at[d - 1],
            dst_ref=rb.at[d - 1],
            send_sem=bal_send.at[d - 1],
            recv_sem=bal_recv.at[d - 1],
            device_id={"group": other},
            device_id_type=MESH,
        )
        c.start()
        sent.append(c)
    for k in range(SEND_CAP):
        bal_ref[grp * SEND_CAP + k] = outgoing(grp, k)

    receive(ef)
    for d, plane, step in ((1, 0, 0), (0, side + 1, 2)):
        a = dot(jnp.concatenate([rf[d, t] for t in range(count)], axis=0), t2[...]).astype(BF16)
        parts = [a[t * ch : (t + 1) * ch] for t in range(count)]
        convolve(y1, plane, w2f, parts, step)

    for j in range(pairs):
        a = dot(jnp.concatenate([up[t, j] for t in range(count)], axis=0), tup[...]).astype(BF16)
        for h in (0, 1):
            parts = [a[t * ch : (t + 1) * ch, h * 256 : (h + 1) * 256] for t in range(count)]
            convolve(y2, 1 + 2 * j + h, w2u, parts, 1)
    receive(eu)
    for d, plane, step, h in ((1, 0, 0, 1), (0, half + 1, 2, 0)):
        a = dot(jnp.concatenate([ru[d, t] for t in range(count)], axis=0), tup[:, h * 256 : (h + 1) * 256]).astype(BF16)
        parts = [a[t * ch : (t + 1) * ch] for t in range(count)]
        convolve(y2, plane, w2u, parts, step)

    for b in range(count):
        done = []
        for x in range(side):
            u = b2
            for p in range(3):
                u = u + y1[b, x + p, p * ch : (p + 1) * ch]
                u = u + y2[b, (x + p + 1) // 2, p * ch : (p + 1) * ch]
            lhs[x * ch : (x + 1) * ch, 0:256] = (live[b] * silu(u)).astype(BF16)
        flat = dot(lhs[0 : side * ch, 0:256], tout[...])
        for x in range(side):
            out_ref[b, :, x * face : (x + 1) * face] = flat[x * ch : (x + 1) * ch].astype(BF16)

    for copies in (ex, ec, ef, eu):
        finish(copies)
    for d, c in enumerate(sent):
        c.wait()
        source = lax.rem(grp + n_group - (d + 1), n_group)
        for k in range(SEND_CAP):
            bal_ref[source * SEND_CAP + k] = rb[d, k]


def local(n_local, n_group, features, neighbours, coarse_dest, *weights):
    count, ch, cells = features.shape
    side = round(cells ** (1 / 3))
    cc = weights[2].shape[0]
    half, face = side // 2, side * side
    pairs = half // 2
    if side + 2 > 16 or half + 2 > 8 or half % 2 or side**3 != cells:
        raise ValueError("side")
    vmem = lambda *shape: pltpu.VMEM(shape, BF16)
    weights = [w.reshape(1, -1) if w.ndim == 1 else w for w in weights]
    whole = pl.BlockSpec(memory_space=pltpu.VMEM)
    smem = pl.BlockSpec(memory_space=pltpu.SMEM)
    return pl.pallas_call(
        functools.partial(kernel, (side, count, ch, cc, n_local, n_group)),
        out_shape=(
            jax.ShapeDtypeStruct(features.shape, BF16),
            jax.ShapeDtypeStruct((n_group * SEND_CAP, cc, half**3), BF16),
        ),
        in_specs=[smem, smem] + [whole] * (1 + len(weights)),
        out_specs=(whole, whole),
        scratch_shapes=[
            vmem(2, count, ch, face),
            vmem(2, count, ch, face),
            vmem(2, count, cc, 128),
            vmem(2, count, cc, 128),
            vmem(2, count, ch, 256),
            vmem(2, count, ch, 256),
            vmem(2, count, ch, 128),
            vmem(2, count, ch, 128),
            vmem(n_group - 1, SEND_CAP, cc, half**3),
            vmem(n_group - 1, SEND_CAP, cc, half**3),
            vmem(face, 256),
            vmem(256, 256),
            vmem(512, 512),
            vmem(128, 128),
            vmem(128, 512),
            vmem(256, face),
            vmem(64 * half, half**3),
            vmem(3 * ch, 9 * ch),
            vmem(3 * cc, 9 * cc),
            vmem(3 * ch, 9 * ch),
            vmem(3 * ch, 9 * ch),
            vmem(side * count * ch, 512),
            vmem(count, pairs + 1, cc, 128),
            pltpu.VMEM((count, side + 2, 3 * ch, 256), F32),
            pltpu.VMEM((count, half + 2, 3 * ch, 256), F32),
            vmem(count, side, ch, 256),
            vmem(count, pairs, cc, 128),
            vmem(count, pairs, ch, 128),
            vmem(count * pairs * 2 * ch, 512),
            vmem(side * count * ch, 256),
            vmem(count, 3, count, ch, 256),
            vmem(count, 2, count, cc, 128),
            pltpu.SemaphoreType.DMA((4, 2)),
            pltpu.SemaphoreType.DMA((4, 2)),
            pltpu.SemaphoreType.DMA((n_group - 1,)),
            pltpu.SemaphoreType.DMA((n_group - 1,)),
        ],
        compiler_params=pltpu.CompilerParams(collective_id=0, has_side_effects=True),
    )(neighbours, coarse_dest, features, *weights)


def solution(mesh):
    slots = P(("group", "local"), None, None)
    return jax.shard_map(
        functools.partial(local, mesh.shape["local"], mesh.shape["group"]),
        mesh=mesh,
        in_specs=(slots, P(("group", "local"), None), P(("group", "local"))) + (P(),) * 10,
        out_specs=(slots, slots),
        check_vma=False,
    )
```
